32 devices in a mesh: row: 4 (over y, core), col: 8 (over z, x).
Axes of the slice: x: 2, y: 2, z: 4, core: 2. Of those that a mesh axis runs over, the one named last changes fastest.
Arguments:
- patches: float32 [32, 64, 2, 128, 128], P('row', 'col'), may hold values from -6 to 6
- right_offset: int32 [32, 64], P('row', 'col'), may hold values from 57 to 112, as said below
- right_width: int32 [32, 64], P('row', 'col'), may hold values from 16 to 64
- down_offset: int32 [32, 64], P('row', 'col'), may hold values from 57 to 112, as said below
- down_width: int32 [32, 64], P('row', 'col'), may hold values from 16 to 64
Outputs:
- blended: float32 [32, 64, 2, 128, 128], P('row', 'col')
- phases: float32 [2, 32, 64], P(None, 'row', 'col')
The draws below stay inside these ranges and needn't reach their ends.
Inputs may be any that keep to these rules, and one draw needn't show every extreme that they name: right_offset + right_width lies above 120 and at most 128. down_offset + down_width lies above 120 and at most 128.
All inputs are finite; a program needn't handle non-finite values.
Results may differ from the reference program's by a relative error of at most 0.0003.
Values sent between devices are 32-bit elements; how exact they have to be, the bound alone decides.
A program may use at most 128 MiB of HBM per device.

```python
import jax
import jax.numpy as jnp
from jax import lax

PATCH = 128
STRIP_MIN = 16
STRIP_MAX = 64
JITTER = 8
ITERS = 2
GRID_ROWS = 32
GRID_COLS = 64


def draw_patches(key, part):
    shape = (GRID_ROWS, GRID_COLS, 2, PATCH, PATCH)
    return jnp.clip(jax.random.normal(jax.random.fold_in(key, 5), shape, jnp.float32), -6.0, 6.0)


def strip_table(key, salt):
    base = jax.random.fold_in(key, salt)
    width_key, jitter_key = jax.random.split(base)
    width = jax.random.randint(width_key, (GRID_ROWS, GRID_COLS), STRIP_MIN, STRIP_MAX + 1)
    jitter = jax.random.randint(jitter_key, (GRID_ROWS, GRID_COLS), 0, JITTER)
    width = width.at[0, 0].set(STRIP_MAX).at[1, 1].set(STRIP_MIN)
    jitter = jitter.at[0, 0].set(JITTER - 1).at[1, 1].set(0)
    return (width.astype(jnp.int32), (PATCH - width - jitter).astype(jnp.int32))


def draw_right_offset(key, part):
    return strip_table(key, 11)[1]


def draw_right_width(key, part):
    return strip_table(key, 11)[0]


def draw_down_offset(key, part):
    return strip_table(key, 23)[1]


def draw_down_width(key, part):
    return strip_table(key, 23)[0]


def setup_inputs(seed: int = 0) -> dict:
    seeds = jax.random.split(jax.random.key(seed), 6)
    return {
        "patches": draw_patches(jax.random.fold_in(seeds[5], 71), 0),
        "right_offset": draw_right_offset(jax.random.fold_in(seeds[5], 71), 0),
        "right_width": draw_right_width(jax.random.fold_in(seeds[5], 71), 0),
        "down_offset": draw_down_offset(jax.random.fold_in(seeds[5], 71), 0),
        "down_width": draw_down_width(jax.random.fold_in(seeds[5], 71), 0),
    }


eps_norm = 1.0

def gather_lanes(field, index, axis):
    return jnp.take_along_axis(field, jnp.broadcast_to(index, field.shape), axis=axis)

def correlate(shifted, partner, width_table):
    real_part = lax.optimization_barrier(jnp.sum(shifted[..., 0, :, :] * partner[..., 0, :, :] + shifted[..., 1, :, :] * partner[..., 1, :, :], axis=(-2, -1)))
    imag_part = lax.optimization_barrier(jnp.sum(shifted[..., 0, :, :] * partner[..., 1, :, :] - shifted[..., 1, :, :] * partner[..., 0, :, :], axis=(-2, -1)))
    scale = 1.0 / jnp.sqrt(PATCH * width_table.astype(jnp.float32))
    return jnp.stack([real_part * scale, imag_part * scale])

def complex_times(factor, field):
    return jnp.stack([factor[0] * field[0] - factor[1] * field[1], factor[0] * field[1] + factor[1] * field[0]])

def conj_times(factor, field):
    return jnp.stack([factor[0] * field[0] + factor[1] * field[1], factor[0] * field[1] - factor[1] * field[0]])

def rotate(factor, field):
    real_part = factor[..., 0:1, :, :] * field[..., 0:1, :, :] - factor[..., 1:2, :, :] * field[..., 1:2, :, :]
    imag_part = factor[..., 0:1, :, :] * field[..., 1:2, :, :] + factor[..., 1:2, :, :] * field[..., 0:1, :, :]
    return jnp.concatenate([real_part, imag_part], axis=-3)

def from_east(field):
    return jnp.pad(field[:, :, 1:], ((0, 0), (0, 0), (0, 1)))

def from_south(field):
    return jnp.pad(field[:, 1:, :], ((0, 0), (0, 1), (0, 0)))

def from_west(field):
    return jnp.pad(field[:, :, :-1], ((0, 0), (0, 0), (1, 0)))

def from_north(field):
    return jnp.pad(field[:, :-1, :], ((0, 0), (1, 0), (0, 0)))

def reference(patches, right_offset, right_width, down_offset, down_width):
    lane_index = jnp.arange(PATCH, dtype=jnp.int32)

    def row_fields(row):
        here = lax.dynamic_index_in_dim(patches, row, 0, False)
        below = lax.dynamic_index_in_dim(patches, jnp.minimum(row + 1, GRID_ROWS - 1).astype(jnp.int32), 0, False)
        below = below * jnp.where(row + 1 < GRID_ROWS, 1.0, 0.0).astype(jnp.float32)
        east = jnp.concatenate([here[1:], jnp.zeros_like(here[:1])], axis=0)
        east_off = lax.dynamic_index_in_dim(right_offset, row, 0, False)
        east_wid = lax.dynamic_index_in_dim(right_width, row, 0, False)
        south_off = lax.dynamic_index_in_dim(down_offset, row, 0, False)
        south_wid = lax.dynamic_index_in_dim(down_width, row, 0, False)
        return (here, below, east, east_off, east_wid, south_off, south_wid)

    def corr_row(row):
        here, below, east, east_off, east_wid, south_off, south_wid = row_fields(row)
        east_index = jnp.clip(lane_index[None, :] + east_off[:, None], 0, PATCH - 1)
        east_keep = (lane_index[None, :] < east_wid[:, None]).astype(jnp.float32)
        east_shifted = gather_lanes(here, east_index[:, None, None, :], 3) * east_keep[:, None, None, :]
        south_index = jnp.clip(lane_index[None, :] + south_off[:, None], 0, PATCH - 1)
        south_keep = (lane_index[None, :] < south_wid[:, None]).astype(jnp.float32)
        south_shifted = gather_lanes(here, south_index[:, None, :, None], 2) * south_keep[:, None, :, None]
        return jnp.concatenate([correlate(east_shifted, east, east_wid), correlate(south_shifted, below, south_wid)])
    rows = jnp.arange(GRID_ROWS, dtype=jnp.int32)
    corr = jnp.transpose(lax.map(corr_row, rows), (1, 0, 2))
    corr_east = corr[0:2]
    corr_south = corr[2:4]
    phase_now = jnp.stack([jnp.ones((GRID_ROWS, GRID_COLS), jnp.float32), jnp.zeros((GRID_ROWS, GRID_COLS), jnp.float32)])
    for step in range(ITERS):
        image = complex_times(corr_east, from_east(phase_now)) + complex_times(corr_south, from_south(phase_now))
        image = image + conj_times(from_west(corr_east), from_west(phase_now)) + conj_times(from_north(corr_south), from_north(phase_now))
        mean_square = jnp.sum(image * image) / (GRID_ROWS * GRID_COLS)
        phase_now = image / jnp.sqrt(mean_square + eps_norm)
    east_phase = from_east(phase_now)
    south_phase = from_south(phase_now)
    col_live = (jnp.arange(GRID_COLS, dtype=jnp.int32) < GRID_COLS - 1).astype(jnp.float32)

    def blend_row(row):
        here, below, east, east_off, east_wid, south_off, south_wid = row_fields(row)
        east_index = jnp.clip(lane_index[None, :] - east_off[:, None], 0, PATCH - 1)
        east_mask = ((lane_index[None, :] >= east_off[:, None]) & (lane_index[None, :] < east_off[:, None] + east_wid[:, None])).astype(jnp.float32)
        east_place = gather_lanes(east, east_index[:, None, None, :], 3) * east_mask[:, None, None, :]
        south_index = jnp.clip(lane_index[None, :] - south_off[:, None], 0, PATCH - 1)
        south_mask = ((lane_index[None, :] >= south_off[:, None]) & (lane_index[None, :] < south_off[:, None] + south_wid[:, None])).astype(jnp.float32)
        south_place = gather_lanes(below, south_index[:, None, :, None], 2) * south_mask[:, None, :, None]
        own = jnp.transpose(lax.dynamic_index_in_dim(phase_now, row, 1, False))[:, :, None, None]
        east_factor = jnp.transpose(lax.dynamic_index_in_dim(east_phase, row, 1, False))[:, :, None, None]
        south_factor = jnp.transpose(lax.dynamic_index_in_dim(south_phase, row, 1, False))[:, :, None, None]
        numer = rotate(own, here) + rotate(east_factor, east_place) + rotate(south_factor, south_place)
        south_live = jnp.where(row + 1 < GRID_ROWS, 1.0, 0.0).astype(jnp.float32)
        weight = 1.0 + (east_mask * col_live[:, None])[:, None, None, :] + (south_mask * south_live)[:, None, :, None]
        return numer / weight
    blended = lax.map(blend_row, rows)
    return (blended, phase_now)
```

```python
import functools

import jax
import jax.numpy as jnp
from jax import lax
from jax.experimental import pallas as pl
from jax.experimental.pallas import tpu as pltpu
from jax.sharding import PartitionSpec as P

ITERS = 2
PAD = 64
eps_norm = 1.0
highest = lax.Precision.HIGHEST
MESH = pl.DeviceIdType.MESH
f32 = jnp.float32


def fold_rows(x):
    return jnp.sum(x, axis=0, keepdims=True)


def pair_rows(a_re, a_im, b_re, b_im):
    return fold_rows(a_re * b_re + a_im * b_im), fold_rows(a_re * b_im - a_im * b_re)


def sync_kernel(
    dims, patches, ro, rw, do, dw, east_out, south_out, phase_out,
    pv, epack, east_recv, south_recv, acc, send_buf, recv, fields,
    col_sem, rest_sem, e_send, e_recv, s_send, s_recv, g_send, g_recv, out_sem,
):
    R, C, S, nr, nc = dims
    H, ndev = S // 2, nr * nc
    lo = H - 8
    span = S - lo
    my_row, my_col = lax.axis_index("row"), lax.axis_index("col")
    me = my_row * nc + my_col

    def coords(d):
        return (d // nc, d % nc)

    barrier = pltpu.get_barrier_semaphore()

    def greet(k, carry):
        pl.semaphore_signal(
            barrier, inc=1, device_id=coords(lax.rem(me + k, ndev)), device_id_type=MESH
        )
        return carry

    lax.fori_loop(1, ndev, greet, 0)

    cols = [
        pltpu.make_async_copy(
            patches.at[pl.ds(i * C * 2 * S, 2 * S)],
            pv.at[pl.ds(PAD + i * C * 2 * S, 2 * S)],
            col_sem.at[i],
        )
        for i in range(R)
    ]
    rests = [
        pltpu.make_async_copy(
            patches.at[pl.ds((i * C + 1) * 2 * S, (C - 1) * 2 * S)],
            pv.at[pl.ds(PAD + (i * C + 1) * 2 * S, (C - 1) * 2 * S)],
            rest_sem.at[i],
        )
        for i in range(R)
    ]
    for copy in cols:
        copy.start()
    for copy in rests:
        copy.start()
    for copy in cols:
        copy.wait()
    lane = lax.broadcasted_iota(jnp.int32, (S, S), 1)

    def pack(i, carry):
        base = pl.multiple_of(PAD + i * C * 2 * S, 8)
        re = pv[pl.ds(base, S), :]
        im = pv[pl.ds(base + S, S), :]
        epack[pl.ds(pl.multiple_of(i * S, 8), S), :] = jnp.where(
            lane < H, re, pltpu.roll(im, H, 1)
        )
        return carry

    lax.fori_loop(0, R, pack, 0)
    acc[...] = jnp.zeros_like(acc)
    pl.semaphore_wait(barrier, ndev - 1)

    def south_copy(k, row):
        return pltpu.make_async_remote_copy(
            src_ref=patches.at[pl.ds(k * S, H)],
            dst_ref=south_recv.at[pl.ds(PAD + k * H, H)],
            send_sem=s_send.at[k],
            recv_sem=s_recv.at[k],
            device_id=(row, my_col),
            device_id_type=MESH,
        )

    def east_copy(k, col):
        return pltpu.make_async_remote_copy(
            src_ref=epack.at[pl.ds(k * S, S)],
            dst_ref=east_recv.at[pl.ds(k * S, S)],
            send_sem=e_send.at[k],
            recv_sem=e_recv.at[k],
            device_id=(my_row, col),
            device_id_type=MESH,
        )

    @pl.when(my_col > 0)
    def _():
        for k in range(R):
            east_copy(k, my_col - 1).start()

    @pl.when(my_row > 0)
    def _():
        for k in range(2 * C):
            south_copy(k, my_row - 1).start()

    for copy in rests:
        copy.wait()

    lane1 = lax.broadcasted_iota(jnp.int32, (1, S), 1)
    rowid = lax.broadcasted_iota(jnp.int32, (span, S), 0) + lo

    def put(plane, p, re, im, width):
        scale = 1.0 / jnp.sqrt(jnp.full((1, S), S * width, jnp.int32).astype(f32))
        acc[pl.ds(plane * R * C + p, 1), :] = re * scale
        acc[pl.ds((plane + 1) * R * C + p, 1), :] = im * scale

    def east_store(i, j, b_re, b_im):
        p = i * C + j
        o, w = ro[i, j], rw[i, j]
        base = pl.multiple_of(PAD + p * 2 * S, 8)
        re, im = pair_rows(pv[pl.ds(base, S), :], pv[pl.ds(base + S, S), :], b_re, b_im)
        keep = (lane1 >= o) & (lane1 < o + w)
        put(0, p, jnp.where(keep, re, 0.0), jnp.where(keep, im, 0.0), w)

    def east_inner(n, carry):
        i, j = n // (C - 1), n % (C - 1)
        o = ro[i, j]
        base = pl.multiple_of(PAD + (i * C + j + 1) * 2 * S, 8)
        east_store(
            i, j,
            pltpu.roll(pv[pl.ds(base, S), :], o, 1),
            pltpu.roll(pv[pl.ds(base + S, S), :], o, 1),
        )
        return carry

    def south_store(i, j, b_re, b_im):
        p = i * C + j
        o, w = do[i, j], dw[i, j]
        base = pl.multiple_of(PAD + p * 2 * S + lo, 8)
        keep = (rowid >= o) & (rowid < o + w)
        re, im = pair_rows(
            pv[pl.ds(base, span), :],
            pv[pl.ds(base + S, span), :],
            jnp.where(keep, b_re, 0.0),
            jnp.where(keep, b_im, 0.0),
        )
        put(2, p, re, im, w)

    def south_inner(p, carry):
        i, j = p // C, p % C
        start = PAD + (p + C) * 2 * S + lo - do[i, j]
        south_store(i, j, pv[pl.ds(start, span), :], pv[pl.ds(start + S, span), :])
        return carry

    lax.fori_loop(0, R * (C - 1), east_inner, 0)
    lax.fori_loop(0, (R - 1) * C, south_inner, 0)

    @pl.when(my_row < nr - 1)
    def _():
        for k in range(2 * C):
            south_copy(k, my_row).wait_recv()

    @pl.when(my_row == nr - 1)
    def _():
        south_recv[...] = jnp.zeros_like(south_recv)

    south_back = pltpu.make_async_copy(
        south_recv.at[pl.ds(PAD, 2 * C * H)], south_out, out_sem.at[0]
    )
    south_back.start()

    def south_edge(j, carry):
        start = PAD + j * 2 * H + lo - do[R - 1, j]
        south_store(
            R - 1, j, south_recv[pl.ds(start, span), :], south_recv[pl.ds(start + H, span), :]
        )
        return carry

    lax.fori_loop(0, C, south_edge, 0)

    @pl.when(my_col < nc - 1)
    def _():
        for k in range(R):
            east_copy(k, my_col).wait_recv()

    @pl.when(my_col == nc - 1)
    def _():
        east_recv[...] = jnp.zeros_like(east_recv)

    east_back = pltpu.make_async_copy(east_recv, east_out, out_sem.at[1])
    east_back.start()

    def east_edge(i, carry):
        o = ro[i, C - 1]
        both = east_recv[pl.ds(pl.multiple_of(i * S, 8), S), :]
        east_store(i, C - 1, pltpu.roll(both, o, 1), pltpu.roll(both, lax.rem(o + H, S), 1))
        return carry

    lax.fori_loop(0, R, east_edge, 0)

    sums = lax.dot_general(
        jnp.ones((8, S), f32), acc[...], (((1,), (1,)), ((), ())),
        precision=highest, preferred_element_type=f32,
    )
    mine = jnp.concatenate([sums[0:1, :S], sums[0:1, S:]], axis=0)
    send_buf[...] = mine
    recv[me] = mine

    def gather_copy(target, source):
        return pltpu.make_async_remote_copy(
            src_ref=send_buf,
            dst_ref=recv.at[source],
            send_sem=g_send.at[target],
            recv_sem=g_recv.at[source],
            device_id=coords(target),
            device_id_type=MESH,
        )

    def spread(k, carry):
        gather_copy(lax.rem(me + k, ndev), me).start()
        return carry

    def collect(k, carry):
        other = lax.rem(me + k, ndev)
        gather_copy(other, other).wait_recv()
        return carry

    def drain(k, carry):
        gather_copy(lax.rem(me + k, ndev), me).wait_send()
        return carry

    lax.fori_loop(1, ndev, spread, 0)
    lax.fori_loop(1, ndev, collect, 0)

    got = recv[...]
    east, south = got[:, 0, :], got[:, 1, :]
    field = lax.broadcasted_iota(jnp.int32, (ndev, S), 0)
    slot = lax.broadcasted_iota(jnp.int32, (ndev, S), 1)
    valid = slot < R * C
    j_of, i_of = slot % C, (slot // C) % R
    dc, dr = field % nc, field // nc

    def roll(x, by, axis):
        return pltpu.roll(x, by % x.shape[axis], axis)

    def from_east(x):
        far = roll(roll(x, -1, 0), C - 1, 1)
        far = jnp.where(dc < nc - 1, far, 0.0)
        return jnp.where(j_of < C - 1, roll(x, -1, 1), far)

    def from_west(x):
        far = roll(roll(x, 1, 0), 1 - C, 1)
        far = jnp.where(dc > 0, far, 0.0)
        return jnp.where(j_of > 0, roll(x, 1, 1), far)

    def from_south(x):
        far = roll(roll(x, -nc, 0), (R - 1) * C, 1)
        far = jnp.where(dr < nr - 1, far, 0.0)
        return jnp.where(i_of < R - 1, roll(x, -C, 1), far)

    def from_north(x):
        far = roll(roll(x, nc, 0), -(R - 1) * C, 1)
        far = jnp.where(dr > 0, far, 0.0)
        return jnp.where(i_of > 0, roll(x, C, 1), far)

    ce = (jnp.where(valid, east, 0.0), jnp.where(valid, roll(east, -R * C, 1), 0.0))
    cs = (jnp.where(valid, south, 0.0), jnp.where(valid, roll(south, -R * C, 1), 0.0))
    cw = tuple(from_west(x) for x in ce)
    cn = tuple(from_north(x) for x in cs)
    count = float(ndev * R * C)

    def times(a, b):
        return (a[0] * b[0] - a[1] * b[1], a[0] * b[1] + a[1] * b[0])

    def conj_times(a, b):
        return (a[0] * b[0] + a[1] * b[1], a[0] * b[1] - a[1] * b[0])

    now = (jnp.ones((ndev, S), f32), jnp.zeros((ndev, S), f32))
    for step in range(ITERS):
        terms = (
            times(ce, tuple(from_east(x) for x in now)),
            times(cs, tuple(from_south(x) for x in now)),
            conj_times(cw, tuple(from_west(x) for x in now)),
            conj_times(cn, tuple(from_north(x) for x in now)),
        )
        image = tuple(
            jnp.where(valid, terms[0][q] + terms[1][q] + terms[2][q] + terms[3][q], 0.0)
            for q in range(2)
        )
        total = jnp.sum(image[0] * image[0] + image[1] * image[1], axis=0, keepdims=True)
        total = jnp.sum(total, axis=1, keepdims=True)
        factor = 1.0 / jnp.sqrt(total / count + eps_norm)
        now = (image[0] * factor, image[1] * factor)
    outs = now + tuple(from_east(x) for x in now) + tuple(from_south(x) for x in now)
    for q in range(6):
        fields[q] = outs[q]
    for q in range(6):
        phase_out[q : q + 1, :] = fields[q, pl.ds(me, 1), :]
    phase_out[6:8, :] = jnp.zeros((2, S), f32)

    lax.fori_loop(1, ndev, drain, 0)

    @pl.when(my_col > 0)
    def _():
        for k in range(R):
            east_copy(k, my_col - 1).wait_send()

    @pl.when(my_row > 0)
    def _():
        for k in range(2 * C):
            south_copy(k, my_row - 1).wait_send()

    south_back.wait()
    east_back.wait()


def blend_kernel(
    dims, patches, east_halo, south_halo, ro, rw, do, dw, g, out, phases,
    pv, ev, sv, ov, in_sem, halo_sem, out_sem,
):
    R, C, S, nr, nc = dims
    H = S // 2
    lo = H - 8
    span = S - lo
    row_size = C * 2 * S
    last_col = lax.axis_index("col") == nc - 1
    last_row = lax.axis_index("row") == nr - 1

    def load(i):
        return pltpu.make_async_copy(
            patches.at[pl.ds(i * row_size, row_size)],
            pv.at[pl.ds(PAD + i * row_size, row_size)],
            in_sem.at[i],
        )

    def save(i):
        return pltpu.make_async_copy(
            ov.at[pl.ds(i * row_size, row_size)],
            out.at[pl.ds(i * row_size, row_size)],
            out_sem.at[i],
        )

    east_load = pltpu.make_async_copy(east_halo, ev, halo_sem.at[0])
    south_load = pltpu.make_async_copy(south_halo, sv.at[pl.ds(PAD, 2 * C * H)], halo_sem.at[1])
    load(0).start()
    east_load.start()
    for i in range(1, R):
        load(i).start()
    south_load.start()

    lane = lax.broadcasted_iota(jnp.int32, (1, S), 1)
    rowid = lax.broadcasted_iota(jnp.int32, (span, S), 0) + lo

    def place(i, j, e_re, e_im, s_re, s_im):
        p = i * C + j
        oe, we, os, ws = ro[i, j], rw[i, j], do[i, j], dw[i, j]
        g_re, g_im = g[0, p], g[1, p]
        ge_re, ge_im, gs_re, gs_im = g[2, p], g[3, p], g[4, p], g[5, p]
        phases[0, i, j] = g_re
        phases[1, i, j] = g_im
        base = pl.multiple_of(PAD + p * 2 * S, 8)
        to = pl.multiple_of(p * 2 * S, 8)
        keep_e = (lane >= oe) & (lane < oe + we)
        live_e = keep_e & jnp.logical_not((j == C - 1) & last_col)
        fe_re = jnp.where(keep_e, ge_re, 0.0)
        fe_im = jnp.where(keep_e, ge_im, 0.0)
        a_re = pv[pl.ds(base, S), :]
        a_im = pv[pl.ds(base + S, S), :]
        n_re = (g_re * a_re - g_im * a_im) + (fe_re * e_re - fe_im * e_im)
        n_im = (g_re * a_im + g_im * a_re) + (fe_re * e_im + fe_im * e_re)
        half = jnp.where(live_e, f32(0.5), f32(1.0))
        third = jnp.where(live_e, f32(1.0 / 3.0), f32(0.5))
        ov[pl.ds(to, lo), :] = n_re[:lo] * half
        ov[pl.ds(pl.multiple_of(to + S, 8), lo), :] = n_im[:lo] * half
        keep_s = (rowid >= os) & (rowid < os + ws)
        p_re = gs_re * s_re - gs_im * s_im
        p_im = gs_re * s_im + gs_im * s_re
        down = jnp.logical_not((i == R - 1) & last_row)
        live_s = keep_s & down
        inv = jnp.where(live_s, third, half)
        ov[pl.ds(pl.multiple_of(to + lo, 8), span), :] = (
            n_re[lo:] + jnp.where(keep_s, p_re, 0.0)
        ) * inv
        ov[pl.ds(pl.multiple_of(to + S + lo, 8), span), :] = (
            n_im[lo:] + jnp.where(keep_s, p_im, 0.0)
        ) * inv

    def east_of(i, j):
        base = pl.multiple_of(PAD + (i * C + j + 1) * 2 * S, 8)
        o = ro[i, j]
        return pltpu.roll(pv[pl.ds(base, S), :], o, 1), pltpu.roll(pv[pl.ds(base + S, S), :], o, 1)

    def east_rim(i):
        o = ro[i, C - 1]
        both = ev[pl.ds(pl.multiple_of(i * S, 8), S), :]
        return pltpu.roll(both, o, 1), pltpu.roll(both, lax.rem(o + H, S), 1)

    def south_of(i, j):
        start = PAD + ((i + 1) * C + j) * 2 * S + lo - do[i, j]
        return pv[pl.ds(start, span), :], pv[pl.ds(start + S, span), :]

    def south_rim(j):
        start = PAD + j * 2 * H + lo - do[R - 1, j]
        return sv[pl.ds(start, span), :], sv[pl.ds(start + H, span), :]

    load(0).wait()
    east_load.wait()

    def rows(i, carry):
        load(i + 1).wait()

        def inner(j, c2):
            place(i, j, *east_of(i, j), *south_of(i, j))
            return c2

        lax.fori_loop(0, C - 1, inner, 0)
        place(i, C - 1, *east_rim(i), *south_of(i, C - 1))
        save(i).start()
        return carry

    lax.fori_loop(0, R - 1, rows, 0)
    south_load.wait()

    def last(j, c2):
        place(R - 1, j, *east_of(R - 1, j), *south_rim(j))
        return c2

    lax.fori_loop(0, C - 1, last, 0)
    place(R - 1, C - 1, *east_rim(R - 1), *south_rim(C - 1))
    save(R - 1).start()
    for i in range(R):
        save(i).wait()


def local(nr, nc, patches, right_offset, right_width, down_offset, down_width):
    R, C, _, S, _ = patches.shape
    H, ndev = S // 2, nr * nc
    dims = (R, C, S, nr, nc)
    flat = patches.reshape(R * C * 2 * S, S)
    anyspec = pl.BlockSpec(memory_space=pl.ANY)
    smem = pl.BlockSpec(memory_space=pltpu.SMEM)
    vmem = pl.BlockSpec(memory_space=pltpu.VMEM)
    dma = pltpu.SemaphoreType.DMA
    tables = (right_offset, right_width, down_offset, down_width)
    east_halo, south_halo, phase = pl.pallas_call(
        functools.partial(sync_kernel, dims),
        out_shape=(
            jax.ShapeDtypeStruct((R * S, S), f32),
            jax.ShapeDtypeStruct((2 * C * H, S), f32),
            jax.ShapeDtypeStruct((8, S), f32),
        ),
        in_specs=[anyspec] + [smem] * 4,
        out_specs=(anyspec, anyspec, vmem),
        scratch_shapes=[
            pltpu.VMEM((PAD + R * C * 2 * S, S), f32),
            pltpu.VMEM((R * S, S), f32),
            pltpu.VMEM((R * S, S), f32),
            pltpu.VMEM((2 * PAD + 2 * C * H, S), f32),
            pltpu.VMEM((4 * R * C, S), f32),
            pltpu.VMEM((2, S), f32),
            pltpu.VMEM((ndev, 2, S), f32),
            pltpu.VMEM((6, ndev, S), f32),
            dma((R,)), dma((R,)),
            dma((R,)), dma((R,)),
            dma((2 * C,)), dma((2 * C,)),
            dma((ndev,)), dma((ndev,)),
            dma((2,)),
        ],
        compiler_params=pltpu.CompilerParams(collective_id=0, has_side_effects=True),
        name="sync_patches",
    )(flat, *tables)
    blended, phases = pl.pallas_call(
        functools.partial(blend_kernel, dims),
        out_shape=(
            jax.ShapeDtypeStruct((R * C * 2 * S, S), f32),
            jax.ShapeDtypeStruct((2, R, C), f32),
        ),
        in_specs=[anyspec] * 3 + [smem] * 5,
        out_specs=(anyspec, smem),
        scratch_shapes=[
            pltpu.VMEM((PAD + R * C * 2 * S, S), f32),
            pltpu.VMEM((R * S, S), f32),
            pltpu.VMEM((2 * PAD + 2 * C * H, S), f32),
            pltpu.VMEM((R * C * 2 * S, S), f32),
            dma((R,)), dma((2,)), dma((R,)),
        ],
        name="blend_patches",
    )(flat, east_halo, south_halo, *tables, phase)
    return blended.reshape(patches.shape), phases


def solution(mesh):
    return jax.shard_map(
        functools.partial(local, mesh.shape["row"], mesh.shape["col"]),
        mesh=mesh,
        in_specs=(P("row", "col", None, None, None),) + (P("row", "col"),) * 4,
        out_specs=(P("row", "col", None, None, None), P(None, "row", "col")),
        check_vma=False,
    )
```

```python
import functools

import jax
import jax.numpy as jnp
from jax import lax
from jax.experimental import pallas as pl
from jax.experimental.pallas import tpu as pltpu
from jax.sharding import PartitionSpec as P

ITERS = 2
PAD = 64
eps_norm = 1.0
highest = lax.Precision.HIGHEST
MESH = pl.DeviceIdType.MESH
f32 = jnp.float32


def fold_rows(x):
    return jnp.sum(x, axis=0, keepdims=True)


def sync_kernel(
    dims, patches, ro, rw, do, dw, east_out, south_out, phase_out,
    pv, epack, east_recv, south_recv, acc, send_buf, recv, fields,
    col_sem, rest_sem, e_send, e_recv, s_send, s_recv, g_send, g_recv, out_sem,
):
    R, C, S, nr, nc = dims
    H, ndev = S // 2, nr * nc
    lo = H - 8
    my_row, my_col = lax.axis_index("row"), lax.axis_index("col")
    me = my_row * nc + my_col

    turn_rows = [lax.rem(my_row + k, nr) for k in range(nr)]
    turn_cols = [lax.rem(my_col + k, nc) for k in range(nc)]
    others = [
        (turn_rows[a], turn_cols[b]) for a in range(nr) for b in range(nc) if a or b
    ]
    barrier = pltpu.get_barrier_semaphore()

    cols = [
        pltpu.make_async_copy(
            patches.at[pl.ds(i * C * 2 * S, 2 * S)],
            pv.at[pl.ds(PAD + i * C * 2 * S, 2 * S)],
            col_sem.at[i],
        )
        for i in range(R)
    ]
    rests = [
        pltpu.make_async_copy(
            patches.at[pl.ds((i * C + 1) * 2 * S, (C - 1) * 2 * S)],
            pv.at[pl.ds(PAD + (i * C + 1) * 2 * S, (C - 1) * 2 * S)],
            rest_sem.at[i],
        )
        for i in range(R)
    ]
    for copy in cols:
        copy.start()
    for other in others:
        pl.semaphore_signal(barrier, inc=1, device_id=other, device_id_type=MESH)
    for copy in rests:
        copy.start()
    for copy in cols:
        copy.wait()
    lane = lax.broadcasted_iota(jnp.int32, (S, S), 1)

    def pack(i, carry):
        base = pl.multiple_of(PAD + i * C * 2 * S, 8)
        re = pv[pl.ds(base, S), :]
        im = pv[pl.ds(base + S, S), :]
        epack[pl.ds(pl.multiple_of(i * S, 8), S), :] = jnp.where(
            lane < H, re, pltpu.roll(im, H, 1)
        )
        return carry

    lax.fori_loop(0, R, pack, 0)
    acc[...] = jnp.zeros_like(acc)
    pl.semaphore_wait(barrier, ndev - 1)

    def south_copy(k, row):
        return pltpu.make_async_remote_copy(
            src_ref=patches.at[pl.ds(k * S, H)],
            dst_ref=south_recv.at[pl.ds(PAD + k * H, H)],
            send_sem=s_send.at[k],
            recv_sem=s_recv.at[k],
            device_id=(row, my_col),
            device_id_type=MESH,
        )

    def east_copy(k, col):
        return pltpu.make_async_remote_copy(
            src_ref=epack.at[pl.ds(k * S, S)],
            dst_ref=east_recv.at[pl.ds(k * S, S)],
            send_sem=e_send.at[k],
            recv_sem=e_recv.at[k],
            device_id=(my_row, col),
            device_id_type=MESH,
        )

    @pl.when(my_col > 0)
    def _():
        for k in range(R):
            east_copy(k, my_col - 1).start()

    @pl.when(my_row > 0)
    def _():
        for k in range(2 * C):
            south_copy(k, my_row - 1).start()

    for copy in rests:
        copy.wait()

    lane1 = lax.broadcasted_iota(jnp.int32, (1, S), 1)
    row8 = lax.broadcasted_iota(jnp.int32, (8, S), 0)

    def put(plane, p, re, im, width):
        scale = 1.0 / jnp.sqrt(jnp.full((1, S), S * width, jnp.int32).astype(f32))
        acc[pl.ds(plane * R * C + p, 1), :] = fold_rows(re) * scale
        acc[pl.ds((plane + 1) * R * C + p, 1), :] = fold_rows(im) * scale

    def gathered(pieces):
        re, im = None, None
        for a_re, a_im, b_re, b_im in pieces:
            u, v = a_re * b_re + a_im * b_im, a_re * b_im - a_im * b_re
            re, im = (u, v) if re is None else (re + u, im + v)
        return re, im

    def east_store(i, j, load_b):
        p = i * C + j
        o, w = ro[i, j], rw[i, j]
        base = PAD + p * 2 * S
        re, im = gathered(
            (pv[pl.ds(pl.multiple_of(base + q, 8), 8), :],
             pv[pl.ds(pl.multiple_of(base + S + q, 8), 8), :]) + load_b(q, o)
            for q in range(0, S, 8)
        )
        keep = (lane1 >= o) & (lane1 < o + w)
        put(0, p, jnp.where(keep, re, 0.0), jnp.where(keep, im, 0.0), w)

    def east_inner(i, carry):
        for j in range(C - 1):
            base = PAD + (i * C + j + 1) * 2 * S

            def load_b(q, o):
                return (
                    pltpu.roll(pv[pl.ds(pl.multiple_of(base + q, 8), 8), :], o, 1),
                    pltpu.roll(pv[pl.ds(pl.multiple_of(base + S + q, 8), 8), :], o, 1),
                )

            east_store(i, j, load_b)
        return carry

    def south_store(i, j, ref, start, gap):
        p = i * C + j
        o, w = do[i, j], dw[i, j]
        base = PAD + p * 2 * S

        def piece(q):
            keep = row8 >= o - q if q < S - 8 else row8 < o + w - q
            b_re = ref[pl.ds(start + (q - o), 8), :]
            b_im = ref[pl.ds(start + gap + (q - o), 8), :]
            return (
                pv[pl.ds(pl.multiple_of(base + q, 8), 8), :],
                pv[pl.ds(pl.multiple_of(base + S + q, 8), 8), :],
                jnp.where(keep, b_re, 0.0),
                jnp.where(keep, b_im, 0.0),
            )

        re, im = gathered(piece(q) for q in range(lo, S, 8))
        put(2, p, re, im, w)

    def south_inner(i, carry):
        for j in range(C):
            south_store(i, j, pv, PAD + ((i + 1) * C + j) * 2 * S, S)
        return carry

    lax.fori_loop(0, R, east_inner, 0)
    lax.fori_loop(0, R - 1, south_inner, 0)

    @pl.when(my_row < nr - 1)
    def _():
        for k in range(2 * C):
            south_copy(k, my_row).wait_recv()

    @pl.when(my_row == nr - 1)
    def _():
        south_recv[...] = jnp.zeros_like(south_recv)

    south_back = pltpu.make_async_copy(
        south_recv.at[pl.ds(PAD, 2 * C * H)], south_out, out_sem.at[0]
    )
    south_back.start()

    for j in range(C):
        south_store(R - 1, j, south_recv, PAD + j * 2 * H, H)

    @pl.when(my_col == nc - 1)
    def _():
        east_recv[...] = jnp.zeros_like(east_recv)

    for i in range(R):

        @pl.when(my_col < nc - 1)
        def _():
            east_copy(i, my_col).wait_recv()

        def load_b(q, o):
            both = east_recv[pl.ds(i * S + q, 8), :]
            return pltpu.roll(both, o, 1), pltpu.roll(both, lax.rem(o + H, S), 1)

        east_store(i, C - 1, load_b)

    sums = lax.dot_general(
        jnp.ones((8, S), f32), acc[...], (((1,), (1,)), ((), ())),
        precision=highest, preferred_element_type=f32,
    )
    mine = jnp.concatenate([sums[0:1, :S], sums[0:1, S:]], axis=0)
    send_buf[...] = mine
    recv[me] = mine

    def index(d):
        return d[0] * nc + d[1]

    def gather_copy(target, source):
        return pltpu.make_async_remote_copy(
            src_ref=send_buf,
            dst_ref=recv.at[index(source)],
            send_sem=g_send.at[index(target)],
            recv_sem=g_recv.at[index(source)],
            device_id=target,
            device_id_type=MESH,
        )

    for other in others:
        gather_copy(other, (my_row, my_col)).start()
    east_back = pltpu.make_async_copy(east_recv, east_out, out_sem.at[1])
    east_back.start()
    for other in others:
        gather_copy(other, other).wait_recv()

    got = recv[...]
    east, south = got[:, 0, :], got[:, 1, :]
    field = lax.broadcasted_iota(jnp.int32, (ndev, S), 0)
    slot = lax.broadcasted_iota(jnp.int32, (ndev, S), 1)
    valid = slot < R * C
    j_of, i_of = slot % C, (slot // C) % R
    dc, dr = field % nc, field // nc

    def roll(x, by, axis):
        return pltpu.roll(x, by % x.shape[axis], axis)

    def from_east(x):
        far = roll(roll(x, -1, 0), C - 1, 1)
        far = jnp.where(dc < nc - 1, far, 0.0)
        return jnp.where(j_of < C - 1, roll(x, -1, 1), far)

    def from_west(x):
        far = roll(roll(x, 1, 0), 1 - C, 1)
        far = jnp.where(dc > 0, far, 0.0)
        return jnp.where(j_of > 0, roll(x, 1, 1), far)

    def from_south(x):
        far = roll(roll(x, -nc, 0), (R - 1) * C, 1)
        far = jnp.where(dr < nr - 1, far, 0.0)
        return jnp.where(i_of < R - 1, roll(x, -C, 1), far)

    def from_north(x):
        far = roll(roll(x, nc, 0), -(R - 1) * C, 1)
        far = jnp.where(dr > 0, far, 0.0)
        return jnp.where(i_of > 0, roll(x, C, 1), far)

    ce = (jnp.where(valid, east, 0.0), jnp.where(valid, roll(east, -R * C, 1), 0.0))
    cs = (jnp.where(valid, south, 0.0), jnp.where(valid, roll(south, -R * C, 1), 0.0))
    cw = tuple(from_west(x) for x in ce)
    cn = tuple(from_north(x) for x in cs)
    count = float(ndev * R * C)

    def times(a, b):
        return (a[0] * b[0] - a[1] * b[1], a[0] * b[1] + a[1] * b[0])

    def conj_times(a, b):
        return (a[0] * b[0] + a[1] * b[1], a[0] * b[1] - a[1] * b[0])

    now = (jnp.ones((ndev, S), f32), jnp.zeros((ndev, S), f32))
    for step in range(ITERS):
        terms = (
            times(ce, tuple(from_east(x) for x in now)),
            times(cs, tuple(from_south(x) for x in now)),
            conj_times(cw, tuple(from_west(x) for x in now)),
            conj_times(cn, tuple(from_north(x) for x in now)),
        )
        image = tuple(
            jnp.where(valid, terms[0][q] + terms[1][q] + terms[2][q] + terms[3][q], 0.0)
            for q in range(2)
        )
        total = jnp.sum(image[0] * image[0] + image[1] * image[1], axis=0, keepdims=True)
        total = jnp.sum(total, axis=1, keepdims=True)
        factor = 1.0 / jnp.sqrt(total / count + eps_norm)
        now = (image[0] * factor, image[1] * factor)
    outs = now + tuple(from_east(x) for x in now) + tuple(from_south(x) for x in now)
    for q in range(6):
        fields[q] = outs[q]
    for q in range(6):
        phase_out[q : q + 1, :] = fields[q, pl.ds(me, 1), :]
    phase_out[6:8, :] = jnp.zeros((2, S), f32)

    for other in others:
        gather_copy(other, (my_row, my_col)).wait_send()

    @pl.when(my_col > 0)
    def _():
        for k in range(R):
            east_copy(k, my_col - 1).wait_send()

    @pl.when(my_row > 0)
    def _():
        for k in range(2 * C):
            south_copy(k, my_row - 1).wait_send()

    south_back.wait()
    east_back.wait()


def blend_kernel(
    dims, patches, east_halo, south_halo, ro, rw, do, dw, g, out, phases,
    pv, ev, sv, ov, in_sem, halo_sem, out_sem,
):
    R, C, S, nr, nc = dims
    H = S // 2
    lo = H - 8
    row_size = C * 2 * S
    last_col = lax.axis_index("col") == nc - 1
    last_row = lax.axis_index("row") == nr - 1

    def load(i):
        return pltpu.make_async_copy(
            patches.at[pl.ds(i * row_size, row_size)],
            pv.at[pl.ds(PAD + i * row_size, row_size)],
            in_sem.at[i],
        )

    def save(i):
        return pltpu.make_async_copy(
            ov.at[pl.ds(i * row_size, row_size)],
            out.at[pl.ds(i * row_size, row_size)],
            out_sem.at[i],
        )

    east_load = pltpu.make_async_copy(east_halo, ev, halo_sem.at[0])
    south_load = pltpu.make_async_copy(south_halo, sv.at[pl.ds(PAD, 2 * C * H)], halo_sem.at[1])
    load(0).start()
    east_load.start()
    for i in range(1, R):
        load(i).start()
    south_load.start()

    lane = lax.broadcasted_iota(jnp.int32, (1, S), 1)
    row8 = lax.broadcasted_iota(jnp.int32, (8, S), 0)

    def at(ref, row):
        return ref[pl.ds(pl.multiple_of(row, 8), 8), :]

    def place(i, j, east, ref, start, gap):
        p = i * C + j
        oe, we, os, ws = ro[i, j], rw[i, j], do[i, j], dw[i, j]
        g_re, g_im = g[0, p], g[1, p]
        ge_re, ge_im, gs_re, gs_im = g[2, p], g[3, p], g[4, p], g[5, p]
        phases[0, i, j] = g_re
        phases[1, i, j] = g_im
        base = PAD + p * 2 * S
        to = p * 2 * S
        keep_e = (lane >= oe) & (lane < oe + we)
        live_e = keep_e & jnp.logical_not((j == C - 1) & last_col)
        half = jnp.where(live_e, f32(0.5), f32(1.0))
        third = jnp.where(live_e, f32(1.0 / 3.0), f32(0.5))
        down = jnp.logical_not((i == R - 1) & last_row)
        third = jnp.where(jnp.full((1, S), down), third, half)
        half, third = jnp.broadcast_to(half, (8, S)), jnp.broadcast_to(third, (8, S))
        e_re = jnp.broadcast_to(jnp.where(keep_e, ge_re, 0.0), (8, S))
        e_im = jnp.broadcast_to(jnp.where(keep_e, ge_im, 0.0), (8, S))
        h_re, h_im, x_re, x_im = g_re * half, g_im * half, e_re * half, e_im * half
        for q in range(0, S, 8):
            a_re, a_im = at(pv, base + q), at(pv, base + S + q)
            b_re, b_im = east(q, oe)
            if q < lo:
                n_re = (h_re * a_re - h_im * a_im) + (x_re * b_re - x_im * b_im)
                n_im = (h_re * a_im + h_im * a_re) + (x_re * b_im + x_im * b_re)
            else:
                keep = row8 >= os - q if q < S - 8 else row8 < os + ws - q
                s_re = ref[pl.ds(start + (q - os), 8), :]
                s_im = ref[pl.ds(start + gap + (q - os), 8), :]
                n_re = (g_re * a_re - g_im * a_im) + (e_re * b_re - e_im * b_im)
                n_im = (g_re * a_im + g_im * a_re) + (e_re * b_im + e_im * b_re)
                inv = jnp.where(keep, third, half)
                n_re = (n_re + jnp.where(keep, gs_re * s_re - gs_im * s_im, 0.0)) * inv
                n_im = (n_im + jnp.where(keep, gs_re * s_im + gs_im * s_re, 0.0)) * inv
            ov[pl.ds(pl.multiple_of(to + q, 8), 8), :] = n_re
            ov[pl.ds(pl.multiple_of(to + S + q, 8), 8), :] = n_im

    def east_of(i, j):
        base = PAD + (i * C + j + 1) * 2 * S

        def east(q, o):
            return pltpu.roll(at(pv, base + q), o, 1), pltpu.roll(at(pv, base + S + q), o, 1)

        return east

    def east_rim(i):
        def east(q, o):
            both = at(ev, i * S + q)
            return pltpu.roll(both, o, 1), pltpu.roll(both, lax.rem(o + H, S), 1)

        return east

    def south_of(i, j):
        return pv, PAD + ((i + 1) * C + j) * 2 * S, S

    def south_rim(j):
        return sv, PAD + j * 2 * H, H

    load(0).wait()
    east_load.wait()

    def rows(i, carry):
        load(i + 1).wait()

        def inner(j, c2):
            place(i, j, east_of(i, j), *south_of(i, j))
            return c2

        lax.fori_loop(0, C - 1, inner, 0)
        place(i, C - 1, east_rim(i), *south_of(i, C - 1))
        save(i).start()
        return carry

    lax.fori_loop(0, R - 1, rows, 0)
    south_load.wait()

    def last(j, c2):
        place(R - 1, j, east_of(R - 1, j), *south_rim(j))
        return c2

    lax.fori_loop(0, C - 1, last, 0)
    place(R - 1, C - 1, east_rim(R - 1), *south_rim(C - 1))
    save(R - 1).start()
    for i in range(R):
        save(i).wait()


def local(nr, nc, patches, right_offset, right_width, down_offset, down_width):
    R, C, _, S, _ = patches.shape
    H, ndev = S // 2, nr * nc
    dims = (R, C, S, nr, nc)
    flat = patches.reshape(R * C * 2 * S, S)
    anyspec = pl.BlockSpec(memory_space=pl.ANY)
    smem = pl.BlockSpec(memory_space=pltpu.SMEM)
    vmem = pl.BlockSpec(memory_space=pltpu.VMEM)
    dma = pltpu.SemaphoreType.DMA
    tables = (right_offset, right_width, down_offset, down_width)
    east_halo, south_halo, phase = pl.pallas_call(
        functools.partial(sync_kernel, dims),
        out_shape=(
            jax.ShapeDtypeStruct((R * S, S), f32),
            jax.ShapeDtypeStruct((2 * C * H, S), f32),
            jax.ShapeDtypeStruct((8, S), f32),
        ),
        in_specs=[anyspec] + [smem] * 4,
        out_specs=(anyspec, anyspec, vmem),
        scratch_shapes=[
            pltpu.VMEM((PAD + R * C * 2 * S, S), f32),
            pltpu.VMEM((R * S, S), f32),
            pltpu.VMEM((R * S, S), f32),
            pltpu.VMEM((2 * PAD + 2 * C * H, S), f32),
            pltpu.VMEM((4 * R * C, S), f32),
            pltpu.VMEM((2, S), f32),
            pltpu.VMEM((ndev, 2, S), f32),
            pltpu.VMEM((6, ndev, S), f32),
            dma((R,)), dma((R,)),
            dma((R,)), dma((R,)),
            dma((2 * C,)), dma((2 * C,)),
            dma((ndev,)), dma((ndev,)),
            dma((2,)),
        ],
        compiler_params=pltpu.CompilerParams(collective_id=0, has_side_effects=True),
        name="sync_patches",
    )(flat, *tables)
    blended, phases = pl.pallas_call(
        functools.partial(blend_kernel, dims),
        out_shape=(
            jax.ShapeDtypeStruct((R * C * 2 * S, S), f32),
            jax.ShapeDtypeStruct((2, R, C), f32),
        ),
        in_specs=[anyspec] * 3 + [smem] * 5,
        out_specs=(anyspec, smem),
        scratch_shapes=[
            pltpu.VMEM((PAD + R * C * 2 * S, S), f32),
            pltpu.VMEM((R * S, S), f32),
            pltpu.VMEM((2 * PAD + 2 * C * H, S), f32),
            pltpu.VMEM((R * C * 2 * S, S), f32),
            dma((R,)), dma((2,)), dma((R,)),
        ],
        name="blend_patches",
    )(flat, east_halo, south_halo, *tables, phase)
    return blended.reshape(patches.shape), phases


def solution(mesh):
    return jax.shard_map(
        functools.partial(local, mesh.shape["row"], mesh.shape["col"]),
        mesh=mesh,
        in_specs=(P("row", "col", None, None, None),) + (P("row", "col"),) * 4,
        out_specs=(P("row", "col", None, None, None), P(None, "row", "col")),
        check_vma=False,
    )
```

```python
import functools

import jax
import jax.numpy as jnp
from jax import lax
from jax.experimental import pallas as pl
from jax.experimental.pallas import tpu as pltpu
from jax.sharding import PartitionSpec as P

ITERS = 2
PAD = 64
eps_norm = 1.0
highest = lax.Precision.HIGHEST
MESH = pl.DeviceIdType.MESH
f32 = jnp.float32


def fold_rows(x):
    return jnp.sum(x, axis=0, keepdims=True)


def sync_kernel(
    dims, patches, ro, rw, do, dw, east_out, south_out, phase_out,
    pv, epack, east_recv, south_recv, acc, send_buf, recv, fields,
    col_sem, rest_sem, e_send, e_recv, s_send, s_recv, g_send, g_recv, out_sem,
):
    R, C, S, nr, nc = dims
    H, ndev = S // 2, nr * nc
    lo = H - 8
    my_row, my_col = lax.axis_index("row"), lax.axis_index("col")
    me = my_row * nc + my_col

    turn_rows = [lax.rem(my_row + k, nr) for k in range(nr)]
    turn_cols = [lax.rem(my_col + k, nc) for k in range(nc)]
    others = [
        (turn_rows[a], turn_cols[b]) for a in range(nr) for b in range(nc) if a or b
    ]
    barrier = pltpu.get_barrier_semaphore()

    cols = [
        pltpu.make_async_copy(
            patches.at[pl.ds(i * C * 2 * S, 2 * S)],
            pv.at[pl.ds(PAD + i * C * 2 * S, 2 * S)],
            col_sem.at[i],
        )
        for i in range(R)
    ]
    rests = [
        pltpu.make_async_copy(
            patches.at[pl.ds((i * C + 1) * 2 * S, (C - 1) * 2 * S)],
            pv.at[pl.ds(PAD + (i * C + 1) * 2 * S, (C - 1) * 2 * S)],
            rest_sem.at[i],
        )
        for i in range(R)
    ]
    for copy in cols:
        copy.start()
    for other in others:
        pl.semaphore_signal(barrier, inc=1, device_id=other, device_id_type=MESH)
    for copy in rests:
        copy.start()
    for copy in cols:
        copy.wait()
    lane = lax.broadcasted_iota(jnp.int32, (S, S), 1)

    def pack(i, carry):
        base = pl.multiple_of(PAD + i * C * 2 * S, 8)
        re = pv[pl.ds(base, S), :]
        im = pv[pl.ds(base + S, S), :]
        epack[pl.ds(pl.multiple_of(i * S, 8), S), :] = jnp.where(
            lane < H, re, pltpu.roll(im, H, 1)
        )
        return carry

    lax.fori_loop(0, R, pack, 0)
    acc[...] = jnp.zeros_like(acc)
    pl.semaphore_wait(barrier, ndev - 1)

    def south_copy(k, row):
        return pltpu.make_async_remote_copy(
            src_ref=patches.at[pl.ds(k * S, H)],
            dst_ref=south_recv.at[pl.ds(PAD + k * H, H)],
            send_sem=s_send.at[k],
            recv_sem=s_recv.at[k],
            device_id=(row, my_col),
            device_id_type=MESH,
        )

    def east_copy(k, col):
        return pltpu.make_async_remote_copy(
            src_ref=epack.at[pl.ds(k * S, S)],
            dst_ref=east_recv.at[pl.ds(k * S, S)],
            send_sem=e_send.at[k],
            recv_sem=e_recv.at[k],
            device_id=(my_row, col),
            device_id_type=MESH,
        )

    @pl.when(my_col > 0)
    def _():
        for k in range(R):
            east_copy(k, my_col - 1).start()

    @pl.when(my_row > 0)
    def _():
        for k in range(2 * C):
            south_copy(k, my_row - 1).start()

    for copy in rests:
        copy.wait()

    lane1 = lax.broadcasted_iota(jnp.int32, (1, S), 1)
    row8 = lax.broadcasted_iota(jnp.int32, (8, S), 0)

    def put(plane, p, re, im, width):
        scale = 1.0 / jnp.sqrt(jnp.full((1, S), S * width, jnp.int32).astype(f32))
        acc[pl.ds(plane * R * C + p, 1), :] = fold_rows(re) * scale
        acc[pl.ds((plane + 1) * R * C + p, 1), :] = fold_rows(im) * scale

    def gathered(pieces):
        re, im = None, None
        for a_re, a_im, b_re, b_im in pieces:
            u, v = a_re * b_re + a_im * b_im, a_re * b_im - a_im * b_re
            re, im = (u, v) if re is None else (re + u, im + v)
        return re, im

    def east_store(i, j, load_b):
        p = i * C + j
        o, w = ro[i, j], rw[i, j]
        base = PAD + p * 2 * S
        re, im = gathered(
            (pv[pl.ds(pl.multiple_of(base + q, 8), 8), :],
             pv[pl.ds(pl.multiple_of(base + S + q, 8), 8), :]) + load_b(q, o)
            for q in range(0, S, 8)
        )
        keep = (lane1 >= o) & (lane1 < o + w)
        put(0, p, jnp.where(keep, re, 0.0), jnp.where(keep, im, 0.0), w)

    def east_inner(i, carry):
        for j in range(C - 1):
            base = PAD + (i * C + j + 1) * 2 * S

            def load_b(q, o):
                return (
                    pltpu.roll(pv[pl.ds(pl.multiple_of(base + q, 8), 8), :], o, 1),
                    pltpu.roll(pv[pl.ds(pl.multiple_of(base + S + q, 8), 8), :], o, 1),
                )

            east_store(i, j, load_b)
        return carry

    def south_store(i, j, ref, start, gap):
        p = i * C + j
        o, w = do[i, j], dw[i, j]
        base = PAD + p * 2 * S

        def piece(q):
            keep = row8 >= o - q if q < S - 8 else row8 < o + w - q
            b_re = ref[pl.ds(start + (q - o), 8), :]
            b_im = ref[pl.ds(start + gap + (q - o), 8), :]
            return (
                pv[pl.ds(pl.multiple_of(base + q, 8), 8), :],
                pv[pl.ds(pl.multiple_of(base + S + q, 8), 8), :],
                jnp.where(keep, b_re, 0.0),
                jnp.where(keep, b_im, 0.0),
            )

        re, im = gathered(piece(q) for q in range(lo, S, 8))
        put(2, p, re, im, w)

    def south_inner(i, carry):
        for j in range(C):
            south_store(i, j, pv, PAD + ((i + 1) * C + j) * 2 * S, S)
        return carry

    lax.fori_loop(0, R, east_inner, 0)
    lax.fori_loop(0, R - 1, south_inner, 0)

    @pl.when(my_row < nr - 1)
    def _():
        for k in range(2 * C):
            south_copy(k, my_row).wait_recv()

    @pl.when(my_row == nr - 1)
    def _():
        south_recv[...] = jnp.zeros_like(south_recv)

    south_back = pltpu.make_async_copy(
        south_recv.at[pl.ds(PAD, 2 * C * H)], south_out, out_sem.at[0]
    )
    south_back.start()

    for j in range(C):
        south_store(R - 1, j, south_recv, PAD + j * 2 * H, H)

    @pl.when(my_col == nc - 1)
    def _():
        east_recv[...] = jnp.zeros_like(east_recv)

    for i in range(R):

        @pl.when(my_col < nc - 1)
        def _():
            east_copy(i, my_col).wait_recv()

        def load_b(q, o):
            both = east_recv[pl.ds(i * S + q, 8), :]
            return pltpu.roll(both, o, 1), pltpu.roll(both, lax.rem(o + H, S), 1)

        east_store(i, C - 1, load_b)

    sums = lax.dot_general(
        jnp.ones((8, S), f32), acc[...], (((1,), (1,)), ((), ())),
        precision=highest, preferred_element_type=f32,
    )
    mine = jnp.concatenate([sums[0:1, :S], sums[0:1, S:]], axis=0)
    send_buf[...] = mine
    recv[me] = mine

    def index(d):
        return d[0] * nc + d[1]

    def gather_copy(target, source):
        return pltpu.make_async_remote_copy(
            src_ref=send_buf,
            dst_ref=recv.at[index(source)],
            send_sem=g_send.at[index(target)],
            recv_sem=g_recv.at[index(source)],
            device_id=target,
            device_id_type=MESH,
        )

    for other in others:
        gather_copy(other, (my_row, my_col)).start()
    east_back = pltpu.make_async_copy(east_recv, east_out, out_sem.at[1])
    east_back.start()
    for other in others:
        gather_copy(other, other).wait_recv()

    got = recv[...]
    east, south = got[:, 0, :], got[:, 1, :]
    field = lax.broadcasted_iota(jnp.int32, (ndev, S), 0)
    slot = lax.broadcasted_iota(jnp.int32, (ndev, S), 1)
    valid = slot < R * C
    j_of, i_of = slot % C, (slot // C) % R
    dc, dr = field % nc, field // nc

    def roll(x, by, axis):
        return pltpu.roll(x, by % x.shape[axis], axis)

    def from_east(x):
        far = roll(roll(x, -1, 0), C - 1, 1)
        far = jnp.where(dc < nc - 1, far, 0.0)
        return jnp.where(j_of < C - 1, roll(x, -1, 1), far)

    def from_west(x):
        far = roll(roll(x, 1, 0), 1 - C, 1)
        far = jnp.where(dc > 0, far, 0.0)
        return jnp.where(j_of > 0, roll(x, 1, 1), far)

    def from_south(x):
        far = roll(roll(x, -nc, 0), (R - 1) * C, 1)
        far = jnp.where(dr < nr - 1, far, 0.0)
        return jnp.where(i_of < R - 1, roll(x, -C, 1), far)

    def from_north(x):
        far = roll(roll(x, nc, 0), -(R - 1) * C, 1)
        far = jnp.where(dr > 0, far, 0.0)
        return jnp.where(i_of > 0, roll(x, C, 1), far)

    ce = (jnp.where(valid, east, 0.0), jnp.where(valid, roll(east, -R * C, 1), 0.0))
    cs = (jnp.where(valid, south, 0.0), jnp.where(valid, roll(south, -R * C, 1), 0.0))
    cw = tuple(from_west(x) for x in ce)
    cn = tuple(from_north(x) for x in cs)
    count = float(ndev * R * C)

    def times(a, b):
        return (a[0] * b[0] - a[1] * b[1], a[0] * b[1] + a[1] * b[0])

    def conj_times(a, b):
        return (a[0] * b[0] + a[1] * b[1], a[0] * b[1] - a[1] * b[0])

    now = (jnp.ones((ndev, S), f32), jnp.zeros((ndev, S), f32))
    for step in range(ITERS):
        terms = (
            times(ce, tuple(from_east(x) for x in now)),
            times(cs, tuple(from_south(x) for x in now)),
            conj_times(cw, tuple(from_west(x) for x in now)),
            conj_times(cn, tuple(from_north(x) for x in now)),
        )
        image = tuple(
            jnp.where(valid, terms[0][q] + terms[1][q] + terms[2][q] + terms[3][q], 0.0)
            for q in range(2)
        )
        total = jnp.sum(image[0] * image[0] + image[1] * image[1], axis=0, keepdims=True)
        total = jnp.sum(total, axis=1, keepdims=True)
        factor = 1.0 / jnp.sqrt(total / count + eps_norm)
        now = (image[0] * factor, image[1] * factor)
    outs = now + tuple(from_east(x) for x in now) + tuple(from_south(x) for x in now)
    for q in range(6):
        fields[q] = outs[q]
    for q in range(6):
        phase_out[q : q + 1, :] = fields[q, pl.ds(me, 1), :]
    phase_out[6:8, :] = jnp.zeros((2, S), f32)

    for other in others:
        gather_copy(other, (my_row, my_col)).wait_send()

    @pl.when(my_col > 0)
    def _():
        for k in range(R):
            east_copy(k, my_col - 1).wait_send()

    @pl.when(my_row > 0)
    def _():
        for k in range(2 * C):
            south_copy(k, my_row - 1).wait_send()

    south_back.wait()
    east_back.wait()


def blend_kernel(
    dims, patches, east_halo, south_halo, ro, rw, do, dw, g, out, phases,
    pv, ev, sv, ov, in_sem, halo_sem, out_sem,
):
    R, C, S, nr, nc = dims
    H = S // 2
    lo = H - 8
    row_size = C * 2 * S
    last_col = lax.axis_index("col") == nc - 1
    last_row = lax.axis_index("row") == nr - 1

    def load(i):
        return pltpu.make_async_copy(
            patches.at[pl.ds(i * row_size, row_size)],
            pv.at[pl.ds(PAD + i * row_size, row_size)],
            in_sem.at[i],
        )

    def save(i):
        return pltpu.make_async_copy(
            ov.at[pl.ds(i * row_size, row_size)],
            out.at[pl.ds(i * row_size, row_size)],
            out_sem.at[i],
        )

    east_load = pltpu.make_async_copy(east_halo, ev, halo_sem.at[0])
    south_load = pltpu.make_async_copy(south_halo, sv.at[pl.ds(PAD, 2 * C * H)], halo_sem.at[1])
    load(0).start()
    east_load.start()
    for i in range(1, R):
        load(i).start()
    south_load.start()

    lane = lax.broadcasted_iota(jnp.int32, (1, S), 1)
    row8 = lax.broadcasted_iota(jnp.int32, (8, S), 0)

    def at(ref, row):
        return ref[pl.ds(pl.multiple_of(row, 8), 8), :]

    def place(i, j, east, ref, start, gap):
        p = i * C + j
        oe, we, os, ws = ro[i, j], rw[i, j], do[i, j], dw[i, j]
        g_re, g_im = g[0, p], g[1, p]
        ge_re, ge_im, gs_re, gs_im = g[2, p], g[3, p], g[4, p], g[5, p]
        phases[0, i, j] = g_re
        phases[1, i, j] = g_im
        base = PAD + p * 2 * S
        to = p * 2 * S
        keep_e = (lane >= oe) & (lane < oe + we)
        live_e = keep_e & jnp.logical_not((j == C - 1) & last_col)
        half = jnp.where(live_e, f32(0.5), f32(1.0))
        third = jnp.where(live_e, f32(1.0 / 3.0), f32(0.5))
        down = jnp.logical_not((i == R - 1) & last_row)
        third = jnp.where(jnp.full((1, S), down), third, half)
        half, third = jnp.broadcast_to(half, (8, S)), jnp.broadcast_to(third, (8, S))
        e_re = jnp.broadcast_to(jnp.where(keep_e, ge_re, 0.0), (8, S))
        e_im = jnp.broadcast_to(jnp.where(keep_e, ge_im, 0.0), (8, S))
        h_re, h_im, x_re, x_im = g_re * half, g_im * half, e_re * half, e_im * half
        for q in range(0, S, 8):
            a_re, a_im = at(pv, base + q), at(pv, base + S + q)
            b_re, b_im = east(q, oe)
            if q < lo:
                n_re = (h_re * a_re - h_im * a_im) + (x_re * b_re - x_im * b_im)
                n_im = (h_re * a_im + h_im * a_re) + (x_re * b_im + x_im * b_re)
            else:
                keep = row8 >= os - q if q < S - 8 else row8 < os + ws - q
                s_re = ref[pl.ds(start + (q - os), 8), :]
                s_im = ref[pl.ds(start + gap + (q - os), 8), :]
                n_re = (g_re * a_re - g_im * a_im) + (e_re * b_re - e_im * b_im)
                n_im = (g_re * a_im + g_im * a_re) + (e_re * b_im + e_im * b_re)
                inv = jnp.where(keep, third, half)
                n_re = (n_re + jnp.where(keep, gs_re * s_re - gs_im * s_im, 0.0)) * inv
                n_im = (n_im + jnp.where(keep, gs_re * s_im + gs_im * s_re, 0.0)) * inv
            ov[pl.ds(pl.multiple_of(to + q, 8), 8), :] = n_re
            ov[pl.ds(pl.multiple_of(to + S + q, 8), 8), :] = n_im

    def east_of(i, j):
        base = PAD + (i * C + j + 1) * 2 * S

        def east(q, o):
            return pltpu.roll(at(pv, base + q), o, 1), pltpu.roll(at(pv, base + S + q), o, 1)

        return east

    def east_rim(i):
        def east(q, o):
            both = at(ev, i * S + q)
            return pltpu.roll(both, o, 1), pltpu.roll(both, lax.rem(o + H, S), 1)

        return east

    def south_of(i, j):
        return pv, PAD + ((i + 1) * C + j) * 2 * S, S

    def south_rim(j):
        return sv, PAD + j * 2 * H, H

    load(0).wait()
    east_load.wait()

    def rows(i, carry):
        load(i + 1).wait()

        for j in range(C):
            place(i, j, east_of(i, j) if j < C - 1 else east_rim(i), *south_of(i, j))
        save(i).start()
        return carry

    lax.fori_loop(0, R - 1, rows, 0)
    south_load.wait()

    for j in range(C):
        place(R - 1, j, east_of(R - 1, j) if j < C - 1 else east_rim(R - 1), *south_rim(j))
    save(R - 1).start()
    for i in range(R):
        save(i).wait()


def local(nr, nc, patches, right_offset, right_width, down_offset, down_width):
    R, C, _, S, _ = patches.shape
    H, ndev = S // 2, nr * nc
    dims = (R, C, S, nr, nc)
    flat = patches.reshape(R * C * 2 * S, S)
    anyspec = pl.BlockSpec(memory_space=pl.ANY)
    smem = pl.BlockSpec(memory_space=pltpu.SMEM)
    vmem = pl.BlockSpec(memory_space=pltpu.VMEM)
    dma = pltpu.SemaphoreType.DMA
    tables = (right_offset, right_width, down_offset, down_width)
    east_halo, south_halo, phase = pl.pallas_call(
        functools.partial(sync_kernel, dims),
        out_shape=(
            jax.ShapeDtypeStruct((R * S, S), f32),
            jax.ShapeDtypeStruct((2 * C * H, S), f32),
            jax.ShapeDtypeStruct((8, S), f32),
        ),
        in_specs=[anyspec] + [smem] * 4,
        out_specs=(anyspec, anyspec, vmem),
        scratch_shapes=[
            pltpu.VMEM((PAD + R * C * 2 * S, S), f32),
            pltpu.VMEM((R * S, S), f32),
            pltpu.VMEM((R * S, S), f32),
            pltpu.VMEM((2 * PAD + 2 * C * H, S), f32),
            pltpu.VMEM((4 * R * C, S), f32),
            pltpu.VMEM((2, S), f32),
            pltpu.VMEM((ndev, 2, S), f32),
            pltpu.VMEM((6, ndev, S), f32),
            dma((R,)), dma((R,)),
            dma((R,)), dma((R,)),
            dma((2 * C,)), dma((2 * C,)),
            dma((ndev,)), dma((ndev,)),
            dma((2,)),
        ],
        compiler_params=pltpu.CompilerParams(collective_id=0, has_side_effects=True),
        name="sync_patches",
    )(flat, *tables)
    blended, phases = pl.pallas_call(
        functools.partial(blend_kernel, dims),
        out_shape=(
            jax.ShapeDtypeStruct((R * C * 2 * S, S), f32),
            jax.ShapeDtypeStruct((2, R, C), f32),
        ),
        in_specs=[anyspec] * 3 + [smem] * 5,
        out_specs=(anyspec, smem),
        scratch_shapes=[
            pltpu.VMEM((PAD + R * C * 2 * S, S), f32),
            pltpu.VMEM((R * S, S), f32),
            pltpu.VMEM((2 * PAD + 2 * C * H, S), f32),
            pltpu.VMEM((R * C * 2 * S, S), f32),
            dma((R,)), dma((2,)), dma((R,)),
        ],
        name="blend_patches",
    )(flat, east_halo, south_halo, *tables, phase)
    return blended.reshape(patches.shape), phases


def solution(mesh):
    return jax.shard_map(
        functools.partial(local, mesh.shape["row"], mesh.shape["col"]),
        mesh=mesh,
        in_specs=(P("row", "col", None, None, None),) + (P("row", "col"),) * 4,
        out_specs=(P("row", "col", None, None, None), P(None, "row", "col")),
        check_vma=False,
    )
```

```python
import functools

import jax
import jax.numpy as jnp
from jax import lax
from jax.experimental import pallas as pl
from jax.experimental.pallas import tpu as pltpu
from jax.sharding import PartitionSpec as P

ITERS = 2
PAD = 64
eps_norm = 1.0
highest = lax.Precision.HIGHEST
MESH = pl.DeviceIdType.MESH
f32 = jnp.float32


def fold_rows(x):
    return jnp.sum(x, axis=0, keepdims=True)


def sync_kernel(
    dims, patches, ro_in, rw_in, do_in, dw_in, pv, east_recv, south_recv, phase_out,
    epack, acc, send_buf, recv, fields, ro, rw, do, dw,
    col_sem, rest_sem, e_send, e_recv, s_send, s_recv, g_send, g_recv, table_sem,
):
    R, C, S, nr, nc = dims
    H, ndev = S // 2, nr * nc
    lo = H - 8
    my_row, my_col = lax.axis_index("row"), lax.axis_index("col")
    me = my_row * nc + my_col

    turn_rows = [lax.rem(my_row + k, nr) for k in range(nr)]
    turn_cols = [lax.rem(my_col + k, nc) for k in range(nc)]
    others = [
        (turn_rows[a], turn_cols[b]) for a in range(nr) for b in range(nc) if a or b
    ]
    barrier = pltpu.get_barrier_semaphore()

    cols = [
        pltpu.make_async_copy(
            patches.at[pl.ds(i * C * 2 * S, 2 * S)],
            pv.at[pl.ds(PAD + i * C * 2 * S, 2 * S)],
            col_sem.at[i],
        )
        for i in range(R)
    ]
    rests = [
        pltpu.make_async_copy(
            patches.at[pl.ds((i * C + 1) * 2 * S, (C - 1) * 2 * S)],
            pv.at[pl.ds(PAD + (i * C + 1) * 2 * S, (C - 1) * 2 * S)],
            rest_sem.at[i],
        )
        for i in range(R)
    ]
    tables = [
        pltpu.make_async_copy(here, there, table_sem.at[k])
        for k, (here, there) in enumerate(zip((ro_in, rw_in, do_in, dw_in), (ro, rw, do, dw)))
    ]
    for copy in cols:
        copy.start()
    for other in others:
        pl.semaphore_signal(barrier, inc=1, device_id=other, device_id_type=MESH)
    for copy in tables:
        copy.start()
    for copy in rests:
        copy.start()
    lane = lax.broadcasted_iota(jnp.int32, (S, S), 1)

    def pack(i):
        base = PAD + i * C * 2 * S
        cols[i].wait()
        re = pv[pl.ds(base, S), :]
        im = pv[pl.ds(base + S, S), :]
        epack[pl.ds(i * S, S), :] = jnp.where(lane < H, re, pltpu.roll(im, H, 1))

    def south_copy(k, row):
        return pltpu.make_async_remote_copy(
            src_ref=patches.at[pl.ds(k * S, H)],
            dst_ref=south_recv.at[pl.ds(PAD + k * H, H)],
            send_sem=s_send.at[k],
            recv_sem=s_recv.at[k],
            device_id=(row, my_col),
            device_id_type=MESH,
        )

    def east_copy(k, col):
        return pltpu.make_async_remote_copy(
            src_ref=epack.at[pl.ds(k * S, S)],
            dst_ref=east_recv.at[pl.ds(k * S, S)],
            send_sem=e_send.at[k],
            recv_sem=e_recv.at[k],
            device_id=(my_row, col),
            device_id_type=MESH,
        )

    def send_east(i):
        @pl.when(my_col > 0)
        def _():
            east_copy(i, my_col - 1).start()

    for i in range(2):
        pack(i)
    pl.semaphore_wait(barrier, ndev - 1)
    for i in range(2):
        send_east(i)

    @pl.when(my_row > 0)
    def _():
        for k in range(2 * C):
            south_copy(k, my_row - 1).start()

    for i in range(2, R):
        pack(i)
        send_east(i)
    acc[...] = jnp.zeros_like(acc)
    for copy in tables:
        copy.wait()
    for copy in rests:
        copy.wait()

    lane1 = lax.broadcasted_iota(jnp.int32, (1, S), 1)
    row8 = lax.broadcasted_iota(jnp.int32, (8, S), 0)

    def put(plane, p, re, im, width):
        scale = 1.0 / jnp.sqrt(jnp.full((1, S), S * width, jnp.int32).astype(f32))
        acc[pl.ds(plane * R * C + p, 1), :] = fold_rows(re) * scale
        acc[pl.ds((plane + 1) * R * C + p, 1), :] = fold_rows(im) * scale

    def gathered(pieces):
        re, im = None, None
        for a_re, a_im, b_re, b_im in pieces:
            u, v = a_re * b_re + a_im * b_im, a_re * b_im - a_im * b_re
            re, im = (u, v) if re is None else (re + u, im + v)
        return re, im

    def east_store(i, j, load_b):
        p = i * C + j
        o, w = ro[i, j], rw[i, j]
        base = PAD + p * 2 * S
        re, im = gathered(
            (pv[pl.ds(pl.multiple_of(base + q, 8), 8), :],
             pv[pl.ds(pl.multiple_of(base + S + q, 8), 8), :]) + load_b(q, o)
            for q in range(0, S, 8)
        )
        keep = (lane1 >= o) & (lane1 < o + w)
        put(0, p, jnp.where(keep, re, 0.0), jnp.where(keep, im, 0.0), w)

    def east_inner(i, carry):
        for j in range(C - 1):
            base = PAD + (i * C + j + 1) * 2 * S

            def load_b(q, o):
                return (
                    pltpu.roll(pv[pl.ds(pl.multiple_of(base + q, 8), 8), :], o, 1),
                    pltpu.roll(pv[pl.ds(pl.multiple_of(base + S + q, 8), 8), :], o, 1),
                )

            east_store(i, j, load_b)
        return carry

    def south_store(i, j, ref, start, gap):
        p = i * C + j
        o, w = do[i, j], dw[i, j]
        base = PAD + p * 2 * S

        def piece(q):
            keep = row8 >= o - q if q < S - 8 else row8 < o + w - q
            b_re = ref[pl.ds(start + (q - o), 8), :]
            b_im = ref[pl.ds(start + gap + (q - o), 8), :]
            return (
                pv[pl.ds(pl.multiple_of(base + q, 8), 8), :],
                pv[pl.ds(pl.multiple_of(base + S + q, 8), 8), :],
                jnp.where(keep, b_re, 0.0),
                jnp.where(keep, b_im, 0.0),
            )

        re, im = gathered(piece(q) for q in range(lo, S, 8))
        put(2, p, re, im, w)

    def south_inner(i, carry):
        for j in range(C):
            south_store(i, j, pv, PAD + ((i + 1) * C + j) * 2 * S, S)
        return carry

    lax.fori_loop(0, R, east_inner, 0)
    lax.fori_loop(0, R - 1, south_inner, 0)

    @pl.when(my_row < nr - 1)
    def _():
        for k in range(2 * C):
            south_copy(k, my_row).wait_recv()

    @pl.when(my_row == nr - 1)
    def _():
        south_recv[...] = jnp.zeros_like(south_recv)

    for j in range(C):
        south_store(R - 1, j, south_recv, PAD + j * 2 * H, H)

    @pl.when(my_col == nc - 1)
    def _():
        east_recv[...] = jnp.zeros_like(east_recv)

    for i in range(R):

        @pl.when(my_col < nc - 1)
        def _():
            east_copy(i, my_col).wait_recv()

        def load_b(q, o):
            both = east_recv[pl.ds(i * S + q, 8), :]
            return pltpu.roll(both, o, 1), pltpu.roll(both, lax.rem(o + H, S), 1)

        east_store(i, C - 1, load_b)

    sums = lax.dot_general(
        jnp.ones((8, S), f32), acc[...], (((1,), (1,)), ((), ())),
        precision=highest, preferred_element_type=f32,
    )
    mine = jnp.concatenate([sums[0:1, :S], sums[0:1, S:]], axis=0)
    send_buf[...] = mine
    recv[me] = mine

    def index(d):
        return d[0] * nc + d[1]

    def gather_copy(target, source):
        return pltpu.make_async_remote_copy(
            src_ref=send_buf,
            dst_ref=recv.at[index(source)],
            send_sem=g_send.at[index(target)],
            recv_sem=g_recv.at[index(source)],
            device_id=target,
            device_id_type=MESH,
        )

    for other in others:
        gather_copy(other, (my_row, my_col)).start()
    for other in others:
        gather_copy(other, other).wait_recv()

    got = recv[...]
    east, south = got[:, 0, :], got[:, 1, :]
    field = lax.broadcasted_iota(jnp.int32, (ndev, S), 0)
    slot = lax.broadcasted_iota(jnp.int32, (ndev, S), 1)
    valid = slot < R * C
    j_of, i_of = slot % C, (slot // C) % R
    dc, dr = field % nc, field // nc

    def roll(x, by, axis):
        return pltpu.roll(x, by % x.shape[axis], axis)

    def from_east(x):
        far = roll(roll(x, -1, 0), C - 1, 1)
        far = jnp.where(dc < nc - 1, far, 0.0)
        return jnp.where(j_of < C - 1, roll(x, -1, 1), far)

    def from_west(x):
        far = roll(roll(x, 1, 0), 1 - C, 1)
        far = jnp.where(dc > 0, far, 0.0)
        return jnp.where(j_of > 0, roll(x, 1, 1), far)

    def from_south(x):
        far = roll(roll(x, -nc, 0), (R - 1) * C, 1)
        far = jnp.where(dr < nr - 1, far, 0.0)
        return jnp.where(i_of < R - 1, roll(x, -C, 1), far)

    def from_north(x):
        far = roll(roll(x, nc, 0), -(R - 1) * C, 1)
        far = jnp.where(dr > 0, far, 0.0)
        return jnp.where(i_of > 0, roll(x, C, 1), far)

    ce = (jnp.where(valid, east, 0.0), jnp.where(valid, roll(east, -R * C, 1), 0.0))
    cs = (jnp.where(valid, south, 0.0), jnp.where(valid, roll(south, -R * C, 1), 0.0))
    cw = tuple(from_west(x) for x in ce)
    cn = tuple(from_north(x) for x in cs)
    count = float(ndev * R * C)

    def times(a, b):
        return (a[0] * b[0] - a[1] * b[1], a[0] * b[1] + a[1] * b[0])

    def conj_times(a, b):
        return (a[0] * b[0] + a[1] * b[1], a[0] * b[1] - a[1] * b[0])

    now = (jnp.ones((ndev, S), f32), jnp.zeros((ndev, S), f32))
    for step in range(ITERS):
        terms = (
            times(ce, tuple(from_east(x) for x in now)),
            times(cs, tuple(from_south(x) for x in now)),
            conj_times(cw, tuple(from_west(x) for x in now)),
            conj_times(cn, tuple(from_north(x) for x in now)),
        )
        image = tuple(
            jnp.where(valid, terms[0][q] + terms[1][q] + terms[2][q] + terms[3][q], 0.0)
            for q in range(2)
        )
        total = jnp.sum(image[0] * image[0] + image[1] * image[1], axis=0, keepdims=True)
        total = jnp.sum(total, axis=1, keepdims=True)
        factor = 1.0 / jnp.sqrt(total / count + eps_norm)
        now = (image[0] * factor, image[1] * factor)
    outs = now + tuple(from_east(x) for x in now) + tuple(from_south(x) for x in now)
    for q in range(6):
        fields[q] = outs[q]
    for q in range(6):
        phase_out[q : q + 1, :] = fields[q, pl.ds(me, 1), :]
    phase_out[6:8, :] = jnp.zeros((2, S), f32)

    for other in others:
        gather_copy(other, (my_row, my_col)).wait_send()

    @pl.when(my_col > 0)
    def _():
        for k in range(R):
            east_copy(k, my_col - 1).wait_send()

    @pl.when(my_row > 0)
    def _():
        for k in range(2 * C):
            south_copy(k, my_row - 1).wait_send()


def blend_kernel(
    dims, pv, ev, sv, ro, rw, do, dw, g, out, phases, ov, out_sem,
):
    R, C, S, nr, nc = dims
    H = S // 2
    lo = H - 8
    row_size = C * 2 * S
    last_col = lax.axis_index("col") == nc - 1
    last_row = lax.axis_index("row") == nr - 1

    def save(i):
        return pltpu.make_async_copy(
            ov.at[pl.ds(i * row_size, row_size)],
            out.at[pl.ds(i * row_size, row_size)],
            out_sem.at[i],
        )

    lane = lax.broadcasted_iota(jnp.int32, (1, S), 1)
    row8 = lax.broadcasted_iota(jnp.int32, (8, S), 0)

    def at(ref, row):
        return ref[pl.ds(pl.multiple_of(row, 8), 8), :]

    def place(i, j, east, ref, start, gap):
        p = i * C + j
        oe, we, os, ws = ro[i, j], rw[i, j], do[i, j], dw[i, j]
        g_re, g_im = g[0, p], g[1, p]
        ge_re, ge_im, gs_re, gs_im = g[2, p], g[3, p], g[4, p], g[5, p]
        phases[0, i, j] = g_re
        phases[1, i, j] = g_im
        base = PAD + p * 2 * S
        to = p * 2 * S
        keep_e = (lane >= oe) & (lane < oe + we)
        live_e = keep_e & jnp.logical_not((j == C - 1) & last_col)
        half = jnp.where(live_e, f32(0.5), f32(1.0))
        third = jnp.where(live_e, f32(1.0 / 3.0), f32(0.5))
        down = jnp.logical_not((i == R - 1) & last_row)
        third = jnp.where(jnp.full((1, S), down), third, half)
        half, third = jnp.broadcast_to(half, (8, S)), jnp.broadcast_to(third, (8, S))
        e_re = jnp.broadcast_to(jnp.where(keep_e, ge_re, 0.0), (8, S))
        e_im = jnp.broadcast_to(jnp.where(keep_e, ge_im, 0.0), (8, S))
        h_re, h_im, x_re, x_im = g_re * half, g_im * half, e_re * half, e_im * half
        for q in range(0, S, 8):
            a_re, a_im = at(pv, base + q), at(pv, base + S + q)
            b_re, b_im = east(q, oe)
            if q < lo:
                n_re = (h_re * a_re - h_im * a_im) + (x_re * b_re - x_im * b_im)
                n_im = (h_re * a_im + h_im * a_re) + (x_re * b_im + x_im * b_re)
            else:
                keep = row8 >= os - q if q < S - 8 else row8 < os + ws - q
                s_re = ref[pl.ds(start + (q - os), 8), :]
                s_im = ref[pl.ds(start + gap + (q - os), 8), :]
                n_re = (g_re * a_re - g_im * a_im) + (e_re * b_re - e_im * b_im)
                n_im = (g_re * a_im + g_im * a_re) + (e_re * b_im + e_im * b_re)
                inv = jnp.where(keep, third, half)
                n_re = (n_re + jnp.where(keep, gs_re * s_re - gs_im * s_im, 0.0)) * inv
                n_im = (n_im + jnp.where(keep, gs_re * s_im + gs_im * s_re, 0.0)) * inv
            ov[pl.ds(pl.multiple_of(to + q, 8), 8), :] = n_re
            ov[pl.ds(pl.multiple_of(to + S + q, 8), 8), :] = n_im

    def east_of(i, j):
        base = PAD + (i * C + j + 1) * 2 * S

        def east(q, o):
            return pltpu.roll(at(pv, base + q), o, 1), pltpu.roll(at(pv, base + S + q), o, 1)

        return east

    def east_rim(i):
        def east(q, o):
            both = at(ev, i * S + q)
            return pltpu.roll(both, o, 1), pltpu.roll(both, lax.rem(o + H, S), 1)

        return east

    def south_of(i, j):
        return pv, PAD + ((i + 1) * C + j) * 2 * S, S

    def south_rim(j):
        return sv, PAD + j * 2 * H, H

    def rows(i, carry):
        for j in range(C):
            place(i, j, east_of(i, j) if j < C - 1 else east_rim(i), *south_of(i, j))
        save(i).start()
        return carry

    lax.fori_loop(0, R - 1, rows, 0)
    for j in range(C):
        place(R - 1, j, east_of(R - 1, j) if j < C - 1 else east_rim(R - 1), *south_rim(j))
    save(R - 1).start()
    for i in range(R):
        save(i).wait()


def local(nr, nc, patches, right_offset, right_width, down_offset, down_width):
    R, C, _, S, _ = patches.shape
    H, ndev = S // 2, nr * nc
    dims = (R, C, S, nr, nc)
    flat = patches.reshape(R * C * 2 * S, S)
    anyspec = pl.BlockSpec(memory_space=pl.ANY)
    smem = pl.BlockSpec(memory_space=pltpu.SMEM)
    vmem = pl.BlockSpec(memory_space=pltpu.VMEM)
    dma = pltpu.SemaphoreType.DMA
    tables = (right_offset, right_width, down_offset, down_width)
    pv, east_halo, south_halo, phase = pl.pallas_call(
        functools.partial(sync_kernel, dims),
        out_shape=(
            pltpu.VMEM((PAD + R * C * 2 * S, S), f32),
            pltpu.VMEM((R * S, S), f32),
            pltpu.VMEM((2 * PAD + 2 * C * H, S), f32),
            jax.ShapeDtypeStruct((8, S), f32),
        ),
        in_specs=[pl.BlockSpec(memory_space=pltpu.HBM)] * 5,
        out_specs=(vmem,) * 4,
        scratch_shapes=[
            pltpu.VMEM((R * S, S), f32),
            pltpu.VMEM((4 * R * C, S), f32),
            pltpu.VMEM((2, S), f32),
            pltpu.VMEM((ndev, 2, S), f32),
            pltpu.VMEM((6, ndev, S), f32),
        ] + [pltpu.SMEM((R, C), jnp.int32)] * 4 + [
            dma((R,)), dma((R,)),
            dma((R,)), dma((R,)),
            dma((2 * C,)), dma((2 * C,)),
            dma((ndev,)), dma((ndev,)),
            dma((4,)),
        ],
        compiler_params=pltpu.CompilerParams(
            collective_id=0, has_side_effects=True, vmem_limit_bytes=16 << 20
        ),
        name="sync_patches",
    )(*(pltpu.with_memory_space_constraint(x, pltpu.HBM) for x in (flat, *tables)))
    blended, phases = pl.pallas_call(
        functools.partial(blend_kernel, dims),
        out_shape=(
            jax.ShapeDtypeStruct((R * C * 2 * S, S), f32),
            jax.ShapeDtypeStruct((2, R, C), f32),
        ),
        in_specs=[vmem] * 3 + [smem] * 5,
        out_specs=(anyspec, smem),
        scratch_shapes=[
            pltpu.VMEM((R * C * 2 * S, S), f32),
            dma((R,)),
        ],
        compiler_params=pltpu.CompilerParams(vmem_limit_bytes=24 << 20),
        name="blend_patches",
    )(pv, east_halo, south_halo, *tables, phase)
    return blended.reshape(patches.shape), phases


def solution(mesh):
    return jax.shard_map(
        functools.partial(local, mesh.shape["row"], mesh.shape["col"]),
        mesh=mesh,
        in_specs=(P("row", "col", None, None, None),) + (P("row", "col"),) * 4,
        out_specs=(P("row", "col", None, None, None), P(None, "row", "col")),
        check_vma=False,
    )
```
